128 devices in a mesh: st: 4 (over y_hi, core), col: 32 (over x, z, y_lo).
Axes of the slice: x: 4, y: 4 (y_hi: 2, y_lo: 2; y = y_hi * 2 + y_lo), z: 4, core: 2. Of those that a mesh axis runs over, the one named last changes fastest.
Arguments:
- forcing: bfloat16 [8, 2048, 8192], P('st', None, 'col'), may hold values from -6 to 6
- operator_rows: bfloat16 [8, 2048, 2048], P('st', 'col'), may hold values from -0.078125 to 0.078125
- counts: int32 [8], P('st'), may hold values from 1 to 3, as said below
- owner_map: int32 [8, 32], P('st'), may hold values from 0 to 31, each once within a row
Outputs:
- adjoint: bfloat16 [8, 2048, 8192], P('st', None, 'col')
The draws below stay inside these ranges and needn't reach their ends.
Inputs may be any that keep to these rules, and one draw needn't show every extreme that they name: `counts`: some station has exactly 3 terms. `owner_map`: each station's row is a permutation of the row blocks.
All inputs are finite; a program needn't handle non-finite values.
Results may differ from the reference program's by a relative error of at most 0.015.
Values may be sent and summed in bfloat16 or wider, within the bound.
No kernel may reach another device: no remote copies, remote signals or barrier semaphores. Data moves between devices by JAX's collectives and lax.ppermute only.
A program may use at most 128 MiB of HBM per device.

```python
import jax
import jax.numpy as jnp
from jax import lax

N = 2048
KMAX = 3
STATIONS = 8
COLS = 8192
OWNERS = 32


def draw_counts(key, part):
    first_key, second_key = jax.random.split(jax.random.fold_in(key, 11))
    base = jax.random.randint(first_key, (STATIONS,), 1, KMAX + 1)
    spot = jax.random.randint(second_key, (), 0, STATIONS)
    return jnp.where(jnp.arange(STATIONS) == spot, KMAX, base).astype(jnp.int32)


def shard_levels(stream_key, shape, cuts, least, largest):
    gain = 1.0
    for position, shards_of in cuts:
        steps = jax.random.uniform(jax.random.fold_in(jax.random.fold_in(stream_key, 6), position), (shards_of,), jnp.float32, least / len(cuts), largest / len(cuts))
        gain = gain * jnp.repeat(jnp.exp(steps), shape[position] // shards_of).reshape((-1,) + (1,) * (len(shape) - 1 - position))
    return gain


def scatter_about(stream_key, dims, width, most, cuts=(), held_as=jnp.bfloat16):
    array = jax.random.normal(stream_key, dims, jnp.float32) * width
    if len(cuts) > 0:
        array = shard_levels(stream_key, dims, cuts, -0.22, 0.18) * array
    return jnp.clip(array, min=-most, max=most).astype(held_as)


def setup_inputs(seed: int = 0) -> dict:
    arg_keys = jax.random.split(jax.random.key(seed), 5)
    forcing = scatter_about(arg_keys[0], (STATIONS, N, COLS), 1.0, 6.0, ((0, 4), (2, 32)))
    operator_rows = scatter_about(arg_keys[1], (STATIONS, N, N), (3 * N) ** -0.5, 0.078125, ((0, 4), (1, 32)))
    counts = draw_counts(jax.random.fold_in(arg_keys[4], 71), 0)
    owner_map = jax.vmap(lambda own: jax.random.permutation(own, OWNERS))(jax.random.split(arg_keys[3], STATIONS)).reshape((STATIONS, OWNERS)).astype(jnp.int32)
    return dict(forcing=forcing, operator_rows=operator_rows, counts=counts, owner_map=owner_map)


def reorder(stored, mapping):
    owners = mapping.shape[0]
    blocks = stored.reshape(owners, stored.shape[0] // owners, stored.shape[1])
    slots = jnp.arange(owners, dtype=jnp.int32)
    inverse = jnp.sum(jnp.where(mapping[None, :] == slots[:, None], slots[None, :], 0), axis=1).astype(jnp.int32)
    return jnp.take(blocks, inverse, axis=0).reshape(stored.shape)


def advance(matrix, incoming, force, count):
    start = (incoming.astype(jnp.float32) + force.astype(jnp.float32)).astype(jnp.bfloat16)

    def power(index, carry):
        phi, total = carry
        phi = jnp.dot(matrix, phi, preferred_element_type=jnp.float32).astype(jnp.bfloat16)
        return phi, total + phi.astype(jnp.float32)

    phi, total = lax.fori_loop(0, count, power, (start, start.astype(jnp.float32)))
    return (0.7 * total).astype(jnp.bfloat16)


def reference(forcing, operator_rows, counts, owner_map):
    def station(carry, items):
        force, stored, count, mapping = items
        matrix = reorder(stored, mapping)
        state = advance(matrix, carry, force, count)
        return state, state

    initial = jnp.zeros((N, COLS), jnp.bfloat16)
    last, states = lax.scan(station, initial, (forcing, operator_rows, counts, owner_map), reverse=True)
    return states
```

```python
import functools

import jax
import jax.numpy as jnp
from jax import lax
from jax.experimental import pallas as pl
from jax.experimental.pallas import tpu as pltpu
from jax.sharding import Mesh, PartitionSpec as P

N = 2048
WIDTH = 256
BLOCK = 64
HALF = 32
TILE = 1024
PIECES = (8, 8, 8, 4, 4, 8, 8, 8, 4, 4)
ST = ("yh", "c")

NEXT = [(i, (i + 1) % 4) for i in range(4)]
PREV = [(i, (i - 1) % 4) for i in range(4)]


def ring(own, axis):
    behind = lax.ppermute(own, axis, NEXT)
    ahead = lax.ppermute(own, axis, PREV)
    n = own.shape[0] // 2
    far_low = lax.ppermute(behind[:n], axis, NEXT)
    far_high = lax.ppermute(ahead[n:], axis, PREV)
    return [own, behind, ahead, far_low, far_high]


def gather(rows):
    across = lax.ppermute(rows, "yl", [(0, 1), (1, 0)])
    pair = jnp.stack([rows, across])
    first = pair[:, :HALF]
    second = pair[:, HALF:]
    first = jnp.concatenate(ring(first, "x"))
    second = jnp.concatenate(ring(second, "z"))
    return ring(first, "z") + ring(second, "x")


def line(items):
    return [(shift, i) for shift in (0, -1, 1, 2) for i in items]


def origins():
    table = []
    for half in (0, 1):
        inner = line([0, 1])
        for outer_shift, (inner_shift, dy) in line(inner):
            if half == 0:
                table.append((half, inner_shift, outer_shift, dy))
            else:
                table.append((half, outer_shift, inner_shift, dy))
    return table


ORIGINS = origins()


def kernel(stations, first, with_result, *refs):
    refs = list(refs)
    pos, counts, owners, forcing = refs[:4]
    at = 4
    pieces = {}
    for s in stations:
        pieces[s] = refs[at : at + len(PIECES)]
        at += len(PIECES)
    incoming = None
    if not first:
        incoming = refs[at]
        at += 1
    if with_result:
        at += 1
    result, outgoing = refs[at : at + 2]
    at += 2
    mat, phi, force, inc, state, dest, mat_sem, in_sem, out_sem = refs[at:]

    @pl.when(pos[3] == 1)
    def _():
        x, z, y = pos[0], pos[1], pos[2]
        in_copies = []
        for n, s in enumerate(stations):
            in_copies.append(pltpu.make_async_copy(forcing.at[s], force.at[n], in_sem.at[n]))
        if not first:
            in_copies.append(pltpu.make_async_copy(incoming, inc, in_sem.at[len(stations)]))
            in_copies[-1].start()
        in_copies[0].start()
        mat_copies = {}
        for n, s in enumerate(stations):
            row = 0
            mat_copies[n] = [[], []]
            for ref, size in zip(pieces[s], PIECES):
                half = row // 32
                copy = pltpu.make_async_copy(ref, mat.at[n, pl.ds(row, size)], mat_sem.at[n, half])
                copy.start()
                mat_copies[n][half].append(copy)
                row += size
            if n + 1 < len(stations):
                in_copies[n + 1].start()
        for n, s in enumerate(stations):
            for i, (half, dx, dz, dy) in enumerate(ORIGINS):
                slot = (lax.rem(x + dx + 4, 4) * 4 + lax.rem(z + dz + 4, 4)) * 2 + lax.rem(y + dy, 2)
                dest[n, i] = owners[s, slot] * BLOCK + half * HALF

        in_copies[0].wait()
        if not first:
            in_copies[len(stations)].wait()
        rows = 256

        def begin(i, c):
            r = pl.ds(pl.multiple_of(i * rows, rows), rows)
            value = force[0, r, :]
            if not first:
                value = (inc[r, :].astype(jnp.float32) + value.astype(jnp.float32)).astype(jnp.bfloat16)
            phi[0, r, :] = value
            return c

        lax.fori_loop(0, N // rows, begin, 0)
        for n, s in enumerate(stations):

            def power(k, c):
                def tile(i, c):
                    @pl.when(k == 0)
                    def _():
                        pltpu.make_async_copy(mat.at[n, pl.ds(0, 32)], mat.at[n, pl.ds(0, 32)], mat_sem.at[n, i]).wait()

                    a = mat[n, pl.ds(pl.multiple_of(i * 32, 32), 32)].reshape(TILE, N)
                    d = jnp.dot(a, phi[k], preferred_element_type=jnp.float32).astype(jnp.bfloat16)
                    for q in range(TILE // HALF):
                        r = pl.multiple_of(dest[n, i * (TILE // HALF) + q], HALF)
                        phi[k + 1, pl.ds(r, HALF), :] = d[q * HALF : (q + 1) * HALF]
                    return c

                return lax.fori_loop(0, N // TILE, tile, c)

            count = counts[s]
            lax.fori_loop(0, count, power, 0)
            more = n + 1 < len(stations)
            if more:
                in_copies[n + 1].wait()

            for terms in (1, 2, 3):

                @pl.when(count == terms)
                def _():
                    def close(i, c):
                        r = pl.ds(pl.multiple_of(i * rows, rows), rows)
                        total = phi[0, r, :].astype(jnp.float32)
                        for k in range(1, terms + 1):
                            total = total + phi[k, r, :].astype(jnp.float32)
                        value = (0.7 * total).astype(jnp.bfloat16)
                        state[n, r, :] = value
                        if more:
                            begun = value.astype(jnp.float32) + force[n + 1, r, :].astype(jnp.float32)
                            phi[0, r, :] = begun.astype(jnp.bfloat16)
                        return c

                    lax.fori_loop(0, N // rows, close, 0)

            pltpu.make_async_copy(state.at[n], result.at[s], out_sem.at[n]).start()
        last = pltpu.make_async_copy(state.at[len(stations) - 1], outgoing, out_sem.at[len(stations)])
        last.start()
        for n, s in enumerate(stations):
            pltpu.make_async_copy(state.at[n], result.at[s], out_sem.at[n]).wait()
        last.wait()


def advance(stations, pos, counts, owners, forcing, pieces, incoming, result):
    first = incoming is None
    operands = [pos, counts, owners, forcing]
    for s in stations:
        operands += pieces[s]
    if not first:
        operands.append(incoming)
    aliases = {}
    if result is not None:
        aliases = {len(operands): 0}
        operands.append(result)
    n = len(stations)
    smem = pl.BlockSpec(memory_space=pltpu.SMEM)
    hbm = pl.BlockSpec(memory_space=pl.ANY)
    return pl.pallas_call(
        functools.partial(kernel, stations, first, result is not None),
        out_shape=(
            jax.ShapeDtypeStruct((2, N, WIDTH), jnp.bfloat16),
            jax.ShapeDtypeStruct((N, WIDTH), jnp.bfloat16),
        ),
        in_specs=[smem] * 3 + [hbm] * (len(operands) - 3),
        out_specs=(hbm, hbm),
        input_output_aliases=aliases,
        scratch_shapes=[
            pltpu.VMEM((n, 64, HALF, N), jnp.bfloat16),
            pltpu.VMEM((4, N, WIDTH), jnp.bfloat16),
            pltpu.VMEM((n, N, WIDTH), jnp.bfloat16),
            pltpu.VMEM((N, WIDTH), jnp.bfloat16),
            pltpu.VMEM((n, N, WIDTH), jnp.bfloat16),
            pltpu.SMEM((n, 64), jnp.int32),
            pltpu.SemaphoreType.DMA((n, 2)),
            pltpu.SemaphoreType.DMA((n + 1,)),
            pltpu.SemaphoreType.DMA((n + 1,)),
        ],
        compiler_params=pltpu.CompilerParams(vmem_limit_bytes=50 * 2**20),
        cost_estimate=pl.CostEstimate(flops=n * 6 * N * N * WIDTH, bytes_accessed=n * 2 * N * N, transcendentals=0),
    )(*operands)


def shards(forcing, operator_rows, counts, owner_map):
    x, z, y = lax.axis_index("x"), lax.axis_index("z"), lax.axis_index("yl")
    place = lax.axis_index("yh") * 2 + lax.axis_index("c")

    def where(turn):
        return jnp.stack([x, z, y, (place == 3 - turn).astype(jnp.int32)])

    pieces = {1: gather(operator_rows[1]), 0: gather(operator_rows[0])}
    fixed = (counts, owner_map, forcing, pieces)
    result, state = advance((1,), where(0), *fixed, None, None)
    result, state = advance((0,), where(0), *fixed, state, result)
    for turn in (1, 2, 3):
        state = lax.ppermute(state, ST, [(4 - turn, 3 - turn)])
        result, state = advance((1, 0), where(turn), *fixed, state, result)
    return result


def solution(mesh):
    fine = Mesh(mesh.devices.reshape(2, 2, 4, 4, 2), ("yh", "c", "x", "z", "yl"))
    col = ("x", "z", "yl")
    in_specs = (P(ST, None, col), P(ST, col, None), P(ST), P(ST, None))
    out_specs = P(ST, None, col)
    return jax.shard_map(shards, mesh=fine, in_specs=in_specs, out_specs=out_specs, check_vma=False)
```
